32 devices in a mesh: tok: 16 (over z, y, core), head: 2 (over x).
Axes of the slice: x: 2, y: 2, z: 4, core: 2. Of those that a mesh axis runs over, the one named last changes fastest.
Arguments:
- hidden: bfloat16 [8192, 5120], P('tok', 'head'), may hold values from -6 to 6
- w_latent: bfloat16 [5120, 512], P('head'), may hold values from -0.078125 to 0.078125
- w_rope: bfloat16 [5120, 64], P('head'), may hold values from -0.078125 to 0.078125
- kv_gain: float32 [512], replicated, may hold values from 0.25 to 1.75
- q_latent: bfloat16 [16, 32, 64, 512], P('tok', None, 'head'), may hold values from -105 to 105
- q_rope: bfloat16 [16, 32, 4096], P('tok', None, 'head'), may hold values from -6 to 6
- w_value: bfloat16 [64, 512, 128], P('head'), may hold values from -0.25 to 0.25
- page_table: int32 [16, 10], replicated, may hold values from -1 to 63, as said below
- dest_group: int32 [16], replicated, may hold values from 0 to 15, each once
- ctx_len: int32 [16], replicated, may hold values from 1 to 1280, as said below
Outputs:
- attn_out: bfloat16 [16, 32, 8192], P('tok', 'head')
The draws below stay inside these ranges and needn't reach their ends.
Inputs may be any that keep to these rules, and one draw needn't show every extreme that they name: `page_table`: row r lists request r's pages in context order, then -1; every page appears in exactly one row; no row holds two pages p whose p // 4 is equal; some row holds 10 pages. Request r's listed pages number ctx_len[r] / 128 rounded up. `dest_group`: every group serves exactly one request.
All inputs are finite; a program needn't handle non-finite values.
Results may differ from the reference program's by a relative error of at most 0.012.
The reference program's roundings to bfloat16 on the way count: a program that leaves them out, or rounds other values in their place, can miss the bound.
Values may be sent and summed in bfloat16 or wider, within the bound.
No kernel may reach another device: no remote copies, remote signals or barrier semaphores. Data moves between devices by JAX's collectives and lax.ppermute only.
A program may use at most 64 MiB of HBM per device.

```python
import jax
import jax.numpy as jnp
from jax import lax

D = 5120
LAT = 512
ROPE = 64
VDIM = 128
H = 64
PAGE = 128
ROWS = 32
BLOCK = 4
PAGES_DEV = 4
GROUPS = 16
TOKENS = 8192
NPAGES = 64
MAXP = 10
MAXPAD = 12


def page_plan(key):
    base_key = jax.random.fold_in(key, 7)
    chosen_key, weight_key, source_key, within_key = jax.random.split(base_key, 4)
    page_count = GROUPS * PAGES_DEV
    chosen = jax.random.randint(chosen_key, (), 0, GROUPS)
    weights = jax.random.randint(weight_key, (GROUPS,), 1, 9)
    request_ids = jnp.arange(GROUPS, dtype=jnp.int32)
    counts = jnp.where(request_ids == chosen, MAXP, 1).astype(jnp.int32)
    surplus = page_count - MAXP - (GROUPS - 1)
    big_score = 1 << 30

    def add_unit(unit_step, counts_now):
        eligible = (request_ids != chosen) & (counts_now < MAXP)
        ranking = jnp.where(eligible, counts_now * 840 // weights * GROUPS + request_ids, big_score)
        winner = jnp.argmin(ranking)
        return counts_now + (request_ids == winner).astype(jnp.int32)
    counts = lax.fori_loop(0, surplus, add_unit, counts)
    source_order = jax.random.permutation(source_key, GROUPS).astype(jnp.int32)
    within_order = jax.vmap(lambda subkey: jax.random.permutation(subkey, PAGES_DEV))(jax.random.split(within_key, GROUPS)).astype(jnp.int32)
    starts = jnp.cumsum(counts) - counts
    column_ids = jnp.arange(MAXP, dtype=jnp.int32)
    entry = jnp.minimum(starts[:, None] + column_ids[None, :], page_count - 1)
    source = source_order[entry % GROUPS]
    local_slot = within_order[source, entry // GROUPS]
    page_rows = jnp.where(column_ids[None, :] < counts[:, None], source * PAGES_DEV + local_slot, -1)
    return (page_rows.astype(jnp.int32), counts)


def draw_page_table(key, part):
    return page_plan(key)[0]


def draw_ctx_len(key, part):
    counts = page_plan(key)[1]
    trimmed = jax.random.randint(jax.random.fold_in(key, 11), (GROUPS,), 0, PAGE)
    return (counts * PAGE - trimmed).astype(jnp.int32)


def draw_q_latent(key, part):
    first_key = jax.random.fold_in(jax.random.fold_in(key, 3), 0)
    full_shape = (GROUPS, ROWS, H, LAT)
    values_drawn = jnp.clip(jax.random.normal(first_key, full_shape, jnp.float32) * 1.5, -9.0, 9.0)
    return values_drawn.astype(jnp.bfloat16)


def steps_of(own_key, dims, cuts, least, high):
    level, own = 1.0, jax.random.fold_in(own_key, 6)
    for axis_at, parts in cuts:
        draws = jnp.exp(jax.random.uniform(jax.random.fold_in(own, axis_at), (parts,), jnp.float32, least / len(cuts), high / len(cuts)))
        level = level * jnp.repeat(draws, dims[axis_at] // parts).reshape([-1 if axis == axis_at else 1 for axis in range(len(dims))])
    return level


def noise(rng, shape, width, bound, pieces=(), kind=jnp.bfloat16):
    array = jax.random.normal(rng, shape, jnp.float32) * width
    if len(pieces) > 0:
        array = steps_of(rng, shape, pieces, -0.22, 0.18) * array
    return jnp.clip(array, min=-bound, max=bound).astype(kind)


def setup_inputs(seed: int = 0) -> dict:
    splits = jax.random.split(jax.random.key(seed), 11)
    hidden = noise(splits[0], (TOKENS, D), 1.0, 6.0, ((0, 16), (1, 2)))
    w_latent = noise(splits[1], (D, LAT), D ** -0.5, 0.078125, ((0, 2),))
    w_rope = noise(splits[2], (D, ROPE), D ** -0.5, 0.078125, ((0, 2),))
    kv_gain = jnp.clip(1.0 + 0.15 * jax.random.normal(splits[3], (LAT,), jnp.float32), 0.25, 1.75)
    q_latent = draw_q_latent(jax.random.fold_in(splits[10], 71), 0)
    q_rope = noise(splits[5], (GROUPS, ROWS, H * ROPE), 1.0, 6.0, ((0, 16), (2, 2)))
    w_value = noise(splits[6], (H, LAT, VDIM), LAT ** -0.5, 0.25, ((0, 2),))
    page_table = draw_page_table(jax.random.fold_in(splits[10], 71), 0)
    dest_group = jax.random.permutation(splits[8], GROUPS).astype(jnp.int32)
    ctx_len = draw_ctx_len(jax.random.fold_in(splits[10], 71), 0)
    return dict(hidden=hidden, w_latent=w_latent, w_rope=w_rope, kv_gain=kv_gain, q_latent=q_latent, q_rope=q_rope, w_value=w_value, page_table=page_table, dest_group=dest_group, ctx_len=ctx_len)


EPS = 1e-06
SCALE = 192.0 ** (-0.5)
THETA = 10000.0
FLOOR = -1e+30

def normalize(latent_sum, kv_gain):
    inverse = lax.rsqrt(lax.optimization_barrier(jnp.mean(latent_sum * latent_sum, axis=-1, keepdims=True)) + EPS)
    return (latent_sum * inverse * kv_gain).astype(jnp.bfloat16)

def rotate_keys(raw_rope):
    page_total, rope_width, page_len = raw_rope.shape
    half_width = rope_width // 2
    frequency = THETA ** (-2.0 * jnp.arange(half_width, dtype=jnp.float32) / rope_width)
    positions = (jnp.arange(page_total, dtype=jnp.int32)[:, None] * page_len + jnp.arange(page_len, dtype=jnp.int32)[None, :]).astype(jnp.float32)
    angles = frequency[None, :, None] * positions[:, None, :]
    cosine = jnp.cos(angles)
    sine_part = jnp.sin(angles)
    values = raw_rope.astype(jnp.float32)
    first_half = values[:, :half_width]
    second = values[:, half_width:]
    rotated = jnp.concatenate([first_half * cosine - second * sine_part, second * cosine + first_half * sine_part], axis=1)
    return rotated.astype(jnp.bfloat16)

def attend(query_latent, query_rope, key_pages, rope_pages, context):
    page_total, page_len, lat_width = key_pages.shape
    flat_keys = key_pages.reshape(page_total * page_len, lat_width).astype(jnp.float32)
    rope_keys = rope_pages.astype(jnp.float32)
    query_main = query_latent.astype(jnp.float32)
    query_side = query_rope.astype(jnp.float32)
    row_count, head_count = (query_latent.shape[0], query_latent.shape[1])
    block_rows = BLOCK * page_len
    blocks_used = (context + block_rows - 1) // block_rows

    def block_step(block_index, state_now):
        running_max, denominator, accumulated = state_now
        key_block = lax.dynamic_slice_in_dim(flat_keys, block_index * block_rows, block_rows, 0)
        rope_block = lax.dynamic_slice_in_dim(rope_keys, block_index * BLOCK, BLOCK, 0)
        scores = jnp.einsum('rhl,kl->rhk', query_main, key_block)
        scores = scores + jnp.einsum('rhe,jek->rhjk', query_side, rope_block).reshape(row_count, head_count, block_rows)
        scores = scores * SCALE
        positions = block_index * block_rows + jnp.arange(block_rows, dtype=jnp.int32)
        scores = jnp.where(positions < context, scores, FLOOR)
        new_max = jnp.maximum(running_max, lax.optimization_barrier(jnp.max(scores, axis=-1)))
        factor = jnp.exp(running_max - new_max)
        probabilities = jnp.exp(scores - new_max[..., None])
        denominator = denominator * factor + lax.optimization_barrier(jnp.sum(probabilities, axis=-1))
        rounded = lax.optimization_barrier(probabilities.astype(jnp.bfloat16)).astype(jnp.float32)
        accumulated = accumulated * factor[..., None] + jnp.einsum('rhk,kl->rhl', rounded, key_block)
        return (new_max, denominator, accumulated)
    start_state = (jnp.full((row_count, head_count), FLOOR, jnp.float32), jnp.zeros((row_count, head_count), jnp.float32), jnp.zeros((row_count, head_count, lat_width), jnp.float32))
    running_max, denominator, accumulated = lax.fori_loop(0, blocks_used, block_step, start_state)
    return (accumulated / denominator[..., None]).astype(jnp.bfloat16)

def reference(hidden, w_latent, w_rope, kv_gain, q_latent, q_rope, w_value, page_table, dest_group, ctx_len):
    latent_sum = jnp.dot(hidden, w_latent, preferred_element_type=jnp.float32)
    latent_cache = lax.optimization_barrier(normalize(latent_sum, kv_gain)).reshape(NPAGES, PAGE, LAT)
    raw_rope = lax.optimization_barrier(jnp.dot(hidden, w_rope, preferred_element_type=jnp.float32).astype(jnp.bfloat16))
    raw_rope = raw_rope.reshape(NPAGES, PAGE, ROPE).transpose(0, 2, 1)
    filler = -jnp.ones((GROUPS, MAXPAD - MAXP), jnp.int32)
    page_rows = jnp.concatenate([page_table.astype(jnp.int32), filler], axis=1)
    value_maps = w_value.astype(jnp.float32)

    def serve_group(group_id):
        served_here = dest_group == group_id
        page_list = lax.optimization_barrier(jnp.sum(jnp.where(served_here[:, None], page_rows, 0), axis=0)).astype(jnp.int32)
        context = jnp.sum(jnp.where(served_here, ctx_len, 0)).astype(jnp.int32)
        safe_list = jnp.clip(page_list, 0, NPAGES - 1)
        key_pages = latent_cache[safe_list]
        rope_pages = rotate_keys(raw_rope[safe_list])
        query_side = q_rope[group_id].reshape(ROWS, H, ROPE)
        attended = attend(q_latent[group_id], query_side, key_pages, rope_pages, context)
        attended = lax.optimization_barrier(attended).astype(jnp.float32)
        mapped = jnp.einsum('rhl,hlv->rhv', attended, value_maps)
        return mapped.astype(jnp.bfloat16).reshape(ROWS, H * VDIM)
    return lax.map(serve_group, jnp.arange(GROUPS, dtype=jnp.int32))
```

```python
import functools

import jax
import jax.numpy as jnp
from jax import lax
from jax.experimental import pallas as pl
from jax.experimental.pallas import tpu as pltpu
from jax.sharding import PartitionSpec as P

PAGE = 128
LANES = 128
EPS = 1e-06
SCALE = 192.0 ** (-0.5)
THETA = 10000.0
FLOOR = -1e30
BF16, F32 = jnp.bfloat16, jnp.float32
VMEM_LIMIT = 56 * 1024 * 1024


def params(semantics=None):
    return pltpu.CompilerParams(dimension_semantics=semantics, vmem_limit_bytes=VMEM_LIMIT)


def nt_dot(a, b):
    return lax.dot_general(a, b, (((1,), (1,)), ((), ())), preferred_element_type=F32)


def project_kernel(share_ref, hid_ref, wl_ref, wr_ref, *out_refs, pages, tokens):
    first = pl.program_id(1) == 0
    chunks = len(out_refs)
    rows = hid_ref[...].reshape(pages * chunks * tokens, hid_ref.shape[-1])
    lat = jnp.dot(rows, wl_ref[...], preferred_element_type=F32)
    rope = jnp.dot(rows, wr_ref[...], preferred_element_type=F32)
    blocks = lat.shape[1] // LANES
    half = tokens // 2
    for page in range(pages):
        for chunk in range(chunks):
            at = (page * chunks + chunk) * tokens
            parts = [lat[at : at + tokens, b * LANES : (b + 1) * LANES] for b in range(blocks)]
            side = jnp.concatenate([rope[at : at + half], rope[at + half : at + tokens]], axis=1)
            block = jnp.concatenate(parts + [side], axis=0)

            @pl.when(first)
            def _(block=block, page=page, chunk=chunk):
                out_refs[chunk][0, page] = block

            @pl.when(jnp.logical_not(first))
            def _(block=block, page=page, chunk=chunk):
                out_refs[chunk][0, page] += block


def project(hidden, w_latent, w_rope, shares, head_count, chunks):
    features = hidden.shape[1]
    pages = hidden.shape[0] // PAGE
    share = PAGE // head_count
    tokens = share // chunks
    depth = next(d for d in (640, 512, 384, 256, 128) if features % d == 0)
    rows = tokens * (w_latent.shape[1] // LANES) + tokens // 2
    count = shares.shape[0]
    view = hidden.reshape(pages, head_count, share, features)
    grid_spec = pltpu.PrefetchScalarGridSpec(
        num_scalar_prefetch=1,
        grid=(count, features // depth),
        in_specs=[
            pl.BlockSpec((pages, 1, share, depth), lambda s, k, which: (0, which[s], 0, k)),
            pl.BlockSpec((depth, w_latent.shape[1]), lambda s, k, which: (k, 0)),
            pl.BlockSpec((depth, w_rope.shape[1]), lambda s, k, which: (k, 0)),
        ],
        out_specs=[pl.BlockSpec((1, pages, rows, LANES), lambda s, k, which: (s, 0, 0, 0))] * chunks,
    )
    flops = 2 * count * pages * share * features * (w_latent.shape[1] + w_rope.shape[1])
    return pl.pallas_call(
        functools.partial(project_kernel, pages=pages, tokens=tokens),
        grid_spec=grid_spec,
        out_shape=[jax.ShapeDtypeStruct((count, pages, rows, LANES), F32)] * chunks,
        compiler_params=params(("arbitrary", "arbitrary")),
        cost_estimate=pl.CostEstimate(
            flops=flops,
            bytes_accessed=2 * features * (count * pages * share + w_latent.shape[1] + LANES),
            transcendentals=0,
        ),
    )(shares, view, w_latent, w_rope)


def finish_kernel(pick_ref, gain_ref, cos_ref, sin_ref, own_ref, *refs, tokens, blocks):
    out_ref, page_ref = refs[-2:]
    terms = refs[:-2]
    pages = own_ref.shape[1]
    lane = lax.broadcasted_iota(jnp.int32, (tokens // 2, LANES), 1)
    low = (lane % 64) < 32
    for page in range(pages):
        def total(lo, hi):
            value = own_ref[0, page, lo:hi]
            for term in terms:
                value = value + term[page, lo:hi]
            return value

        parts = [total(b * tokens, (b + 1) * tokens) for b in range(blocks)]
        square = parts[0] * parts[0]
        for part in parts[1:]:
            square = square + part * part
        mean = jnp.sum(square, axis=1, keepdims=True) * (1.0 / (blocks * LANES))
        inverse = lax.rsqrt(mean + EPS)
        for b, part in enumerate(parts):
            scaled = part * inverse * gain_ref[b : b + 1]
            page_ref[page, b * tokens : (b + 1) * tokens] = scaled.astype(BF16)
        raw = total(blocks * tokens, blocks * tokens + tokens // 2).astype(BF16).astype(F32)
        other = jnp.where(low, pltpu.roll(raw, LANES - 32, 1), pltpu.roll(raw, 32, 1))
        turned = raw * cos_ref[page] + other * sin_ref[page]
        page_ref[page, blocks * tokens :] = turned.astype(BF16)
    for group in range(out_ref.shape[0]):
        out_ref[group] = page_ref[pick_ref[group]]


def finish(pick, gain, cosine, sine, own, terms, groups, tokens):
    _, pages, rows, _ = own.shape
    blocks = gain.shape[0]
    vmem = pl.BlockSpec(memory_space=pltpu.VMEM)
    return pl.pallas_call(
        functools.partial(finish_kernel, tokens=tokens, blocks=blocks),
        in_specs=[pl.BlockSpec(memory_space=pltpu.SMEM)] + [vmem] * (4 + len(terms)),
        out_specs=vmem,
        out_shape=jax.ShapeDtypeStruct((groups, rows, LANES), BF16),
        scratch_shapes=[pltpu.VMEM((pages, rows, LANES), BF16)],
        compiler_params=params(),
    )(pick, gain, cosine, sine, own, *terms)


def select_kernel(source_ref, in_ref, out_ref):
    for slot in range(out_ref.shape[0]):
        out_ref[slot] = in_ref[source_ref[slot]]


def select(sources, arrived):
    vmem = pl.BlockSpec(memory_space=pltpu.VMEM)
    return pl.pallas_call(
        select_kernel,
        in_specs=[pl.BlockSpec(memory_space=pltpu.SMEM), vmem],
        out_specs=vmem,
        out_shape=jax.ShapeDtypeStruct((sources.shape[0],) + arrived.shape[1:], BF16),
        compiler_params=params(),
    )(sources, arrived)


def attend_kernel(
    meta_ref, q_ref, qr_ref, w_ref, *refs, slots, heads_total, chunks, tokens, blocks, rows_q, step
):
    payloads = refs[: heads_total * chunks]
    out_ref, key_ref, side_ref, score_ref, acc_ref = refs[heads_total * chunks :]
    context = meta_ref[0]
    share = tokens * chunks
    half = tokens // 2

    @pl.when(pl.program_id(0) == 0)
    def _():
        for plane in range(heads_total):
            for chunk in range(chunks):
                payload = payloads[plane * chunks + chunk]
                offset = meta_ref[1 + plane] * share + chunk * tokens

                def fill(slot, _, payload=payload, offset=offset):
                    at = pl.multiple_of(slot * PAGE + offset, tokens)
                    for b in range(blocks):
                        key_ref[pl.ds(at, tokens), b * LANES : (b + 1) * LANES] = payload[
                            slot, b * tokens : (b + 1) * tokens
                        ]
                    packed = payload[slot, blocks * tokens :].astype(F32)
                    swapped = pltpu.roll(packed, 64, 1)
                    side_ref[pl.ds(at, tokens)] = jnp.concatenate([packed, swapped], axis=0).astype(BF16)
                    return 0

                lax.fori_loop(0, slots, fill, 0)

    steps = lax.div(context + (step - 1), step)
    query = q_ref[...].reshape(-1, q_ref.shape[-1])
    side_query = qr_ref[...].reshape(-1, LANES)
    count = query.shape[0]

    def score_step(i, top):
        at = pl.multiple_of(i * step, step)
        scores = nt_dot(query, key_ref[pl.ds(at, step)]) + nt_dot(side_query, side_ref[pl.ds(at, step)])
        position = at + lax.broadcasted_iota(jnp.int32, (count, step), 1)
        scores = jnp.where(position < context, scores * SCALE, FLOOR)
        score_ref[i] = scores
        return jnp.maximum(top, jnp.max(scores, axis=1, keepdims=True))

    top = lax.fori_loop(0, steps, score_step, jnp.full((count, 1), FLOOR, F32))
    acc_ref[...] = jnp.zeros_like(acc_ref)

    def value_step(i, total):
        at = pl.multiple_of(i * step, step)
        weights = jnp.exp(score_ref[i] - top)
        acc_ref[...] += jnp.dot(weights.astype(BF16), key_ref[pl.ds(at, step)], preferred_element_type=F32)
        return total + jnp.sum(weights, axis=1, keepdims=True)

    total = lax.fori_loop(0, steps, value_step, jnp.zeros((count, 1), F32))
    attended = (acc_ref[...] / total).astype(BF16)
    for head in range(count // rows_q):
        mapped = jnp.dot(
            attended[head * rows_q : (head + 1) * rows_q], w_ref[head], preferred_element_type=F32
        )
        out_ref[:, head * LANES : (head + 1) * LANES] = mapped.astype(BF16)


def attend(meta, q_latent, q_side, w_value, payloads, heads_total, chunks, tokens):
    heads, rows_q, lat = q_latent.shape
    slots = payloads[0].shape[0]
    per_step = min(8, heads)
    step = 2 * PAGE if slots % 2 == 0 else PAGE
    keys = slots * PAGE
    vmem = pl.BlockSpec(memory_space=pltpu.VMEM)
    grid_spec = pltpu.PrefetchScalarGridSpec(
        num_scalar_prefetch=1,
        grid=(heads // per_step,),
        in_specs=[
            pl.BlockSpec((per_step, rows_q, lat), lambda i, meta: (i, 0, 0)),
            pl.BlockSpec((per_step, rows_q, LANES), lambda i, meta: (i, 0, 0)),
            pl.BlockSpec((per_step,) + w_value.shape[1:], lambda i, meta: (i, 0, 0)),
        ]
        + [vmem] * len(payloads),
        out_specs=pl.BlockSpec((rows_q, per_step * LANES), lambda i, meta: (0, i)),
        scratch_shapes=[
            pltpu.VMEM((keys, lat), BF16),
            pltpu.VMEM((keys, LANES), BF16),
            pltpu.VMEM((keys // step, per_step * rows_q, step), F32),
            pltpu.VMEM((per_step * rows_q, lat), F32),
        ],
    )
    return pl.pallas_call(
        functools.partial(
            attend_kernel,
            slots=slots,
            heads_total=heads_total,
            chunks=chunks,
            tokens=tokens,
            blocks=lat // LANES,
            rows_q=rows_q,
            step=step,
        ),
        grid_spec=grid_spec,
        out_shape=jax.ShapeDtypeStruct((rows_q, heads * LANES), BF16),
        compiler_params=params(("arbitrary",)),
    )(meta, q_latent, q_side, w_value, *payloads)


def shift(value, axis, by):
    count = lax.axis_size(axis)
    return lax.ppermute(value, axis, [(i, (i + by) % count) for i in range(count)])


CHUNKS = 2


def per_device(
    hidden, w_latent, w_rope, kv_gain, q_latent, q_rope, w_value, page_table, dest_group, ctx_len
):
    groups, heads_total = lax.axis_size("tok"), lax.axis_size("head")
    me, my_head = lax.axis_index("tok"), lax.axis_index("head")
    pages = hidden.shape[0] // PAGE
    share = PAGE // heads_total
    chunks = CHUNKS if share // CHUNKS >= 16 else 1
    tokens = share // chunks
    blocks = w_latent.shape[1] // LANES
    others = [(my_head + d) % heads_total for d in range(1, heads_total)]

    sent = project(hidden, w_latent, w_rope, jnp.stack(others).astype(jnp.int32), heads_total, chunks)
    arrived = [
        [shift(sent[c][d - 1], "head", d) for d in range(1, heads_total)] for c in range(chunks)
    ]
    own = project(hidden, w_latent, w_rope, my_head[None].astype(jnp.int32), heads_total, chunks)

    group_ids = jnp.arange(groups, dtype=jnp.int32)
    served = dest_group[None, :] == group_ids[:, None]
    lists = jnp.sum(jnp.where(served[:, :, None], page_table[None], 0), axis=1)
    origin = jnp.where(lists >= 0, lists // pages, -1)
    pick = jnp.sum(jnp.where(origin == me, lists - me * pages, 0), axis=1).astype(jnp.int32)
    page_ids = me * pages + jnp.arange(pages, dtype=jnp.int32)
    slot_ids = jnp.arange(page_table.shape[1], dtype=jnp.int32)
    slot_of = jnp.sum(
        jnp.where(lists[None] == page_ids[:, None, None], slot_ids[None, None, :], 0), axis=(1, 2)
    )
    mine = jnp.sum(jnp.where(group_ids[:, None] == me, origin, 0), axis=0)
    sources = jnp.maximum(mine, 0).astype(jnp.int32)
    context = jnp.sum(jnp.where(dest_group == me, ctx_len, 0)).astype(jnp.int32)

    rope_width = w_rope.shape[1]
    half_width = rope_width // 2
    frequency = THETA ** (-2.0 * jnp.arange(half_width, dtype=F32) / rope_width)
    lane = jnp.arange(LANES, dtype=jnp.int32)
    lane_frequency = jnp.tile(frequency, LANES // half_width)
    sign = jnp.where(lane % rope_width < half_width, -1.0, 1.0).astype(F32)
    row = jnp.arange(tokens // 2, dtype=jnp.int32)
    inside = row[:, None] + (lane // rope_width)[None, :] * (tokens // 2)
    tables = []
    for c in range(chunks):
        position = slot_of[:, None, None] * PAGE + my_head * share + c * tokens + inside[None]
        angle = lane_frequency[None, None, :] * position.astype(F32)
        tables.append((jnp.cos(angle), jnp.sin(angle) * sign))

    rows_q, heads = q_latent.shape[1], q_latent.shape[2]
    query = q_latent[0].transpose(1, 0, 2)
    query_side = q_rope[0].reshape(rows_q, heads, rope_width).transpose(1, 0, 2)
    query_side = jnp.pad(query_side, ((0, 0), (0, 0), (0, LANES - rope_width)))

    gain = kv_gain.reshape(blocks, LANES)
    picked = []
    for c in range(chunks):
        slots = finish(pick, gain, *tables[c], own[c], arrived[c], groups, tokens)
        received = lax.all_to_all(slots, "tok", split_axis=0, concat_axis=0, tiled=True)
        picked.append(select(sources, received))
    payloads = list(picked)
    for d in range(1, heads_total):
        payloads += [shift(picked[c], "head", d) for c in range(chunks)]
    planes = [(my_head - d) % heads_total for d in range(heads_total)]
    meta = jnp.stack([context] + planes).astype(jnp.int32)
    mapped = attend(meta, query, query_side, w_value, payloads, heads_total, chunks, tokens)

    owned = rows_q // heads_total
    width = mapped.shape[1]
    out = jnp.zeros((owned, width * heads_total), BF16)
    for d in range(heads_total):
        piece = lax.dynamic_slice_in_dim(mapped, ((my_head + d) % heads_total) * owned, owned, 0)
        if d > 0:
            piece = shift(piece, "head", d)
        out = lax.dynamic_update_slice(out, piece, (0, ((my_head - d) % heads_total) * width))
    return out[None]


def solution(mesh):
    placed = (
        P("tok", "head"),
        P("head", None),
        P("head", None),
        P(),
        P("tok", None, "head", None),
        P("tok", None, "head"),
        P("head", None, None),
        P(),
        P(),
        P(),
    )
    return jax.shard_map(
        per_device, mesh=mesh, in_specs=placed, out_specs=P("tok", "head", None), check_vma=False
    )
```

```python
import functools

import jax
import jax.numpy as jnp
import numpy as np
from jax import lax
from jax.experimental import pallas as pl
from jax.experimental.pallas import tpu as pltpu
from jax.sharding import PartitionSpec as P


PAGE = 128
LANES = 128
EPS = 1e-06
SCALE = 192.0 ** (-0.5)
THETA = 10000.0
LOG2E = 1.4426950408889634
FLOOR = -1e30
BF16, F32 = jnp.bfloat16, jnp.float32


MIB = 1024 * 1024


def params(mib):
    return pltpu.CompilerParams(vmem_limit_bytes=mib * MIB)


def nt_dot(a, b):
    return lax.dot_general(a, b, (((1,), (1,)), ((), ())), preferred_element_type=F32)


def project_kernel(
    share_ref, hid_ref, wl_ref, wr_ref, *refs, chunks, pages, tokens, parts, shares
):
    outs, (hid_buf, wl_buf, wr_buf, sems) = refs[:chunks], refs[chunks:]
    share = tokens * chunks
    half = tokens // 2
    depth = hid_ref.shape[-1] // parts
    copies = []
    for k in range(parts):
        at = pl.ds(k * depth, depth)
        copies.append(
            [
                pltpu.make_async_copy(wl_ref.at[at], wl_buf.at[at], sems.at[0, k]),
                pltpu.make_async_copy(wr_ref.at[:, at], wr_buf.at[:, at], sems.at[1, k]),
            ]
            + [
                pltpu.make_async_copy(
                    hid_ref.at[:, share_ref[s], :, at], hid_buf.at[s, :, :, at], sems.at[2 + s, k]
                )
                for s in range(shares)
            ]
        )
    for group in copies:
        for copy in group:
            copy.start()
    for s in range(shares):
        lat = rope = None
        for k in range(parts):
            for copy in copies[k] if s == 0 else ():
                copy.wait()
            rows = hid_buf[s, :, :, k * depth : (k + 1) * depth].reshape(pages * share, depth)
            wide = jnp.dot(rows, wl_buf[k * depth : (k + 1) * depth], preferred_element_type=F32)
            side = nt_dot(rows, wr_buf[:, k * depth : (k + 1) * depth])
            lat, rope = (wide, side) if k == 0 else (lat + wide, rope + side)
        blocks = lat.shape[1] // LANES
        for page in range(pages):
            for c in range(chunks):
                at = (page * chunks + c) * tokens
                for b in range(blocks):
                    outs[c][s, page, b * tokens : (b + 1) * tokens] = lat[
                        at : at + tokens, b * LANES : (b + 1) * LANES
                    ]
                outs[c][s, page, blocks * tokens :] = jnp.concatenate(
                    [rope[at : at + half], rope[at + half : at + tokens]], axis=1
                )


def project(hidden, w_latent, w_rope, shares, head_count, chunks):
    features = hidden.shape[1]
    pages = hidden.shape[0] // PAGE
    share = PAGE // head_count
    tokens = share // chunks
    parts = next(n for n in (5, 4, 2, 1) if features % (n * LANES) == 0)
    rows = tokens * (w_latent.shape[1] // LANES) + tokens // 2
    count = shares.shape[0]
    view = hidden.reshape(pages, head_count, share, features)
    side = w_rope.T
    hbm = pl.BlockSpec(memory_space=pltpu.HBM)
    flops = 2 * count * pages * share * features * (w_latent.shape[1] + w_rope.shape[1])
    return pl.pallas_call(
        functools.partial(
            project_kernel, chunks=chunks, pages=pages, tokens=tokens, parts=parts, shares=count
        ),
        in_specs=[pl.BlockSpec(memory_space=pltpu.SMEM), hbm, hbm, hbm],
        out_specs=[pl.BlockSpec(memory_space=pltpu.VMEM)] * chunks,
        out_shape=[jax.ShapeDtypeStruct((count, pages, rows, LANES), F32)] * chunks,
        scratch_shapes=[
            pltpu.VMEM((count, pages, share, features), BF16),
            pltpu.VMEM(w_latent.shape, BF16),
            pltpu.VMEM(side.shape, BF16),
            pltpu.SemaphoreType.DMA((2 + count, parts)),
        ],
        compiler_params=params(63),
        cost_estimate=pl.CostEstimate(
            flops=flops,
            bytes_accessed=2 * features * (count * pages * share + w_latent.shape[1] + LANES),
            transcendentals=0,
        ),
    )(shares, view, w_latent, side)


def request_of(dest_ref, group):
    def look(i, found):
        return jnp.where(dest_ref[i] == group, i, found)

    return lax.fori_loop(0, dest_ref.shape[0], look, 0)


def finish_kernel(dest_ref, table_ref, gain_ref, freq_ref, own_ref, *refs, tokens, blocks, chunk, share):
    terms, outs, page_ref = refs[:-3], refs[-3:-1], refs[-1]
    me, head = lax.axis_index("tok"), lax.axis_index("head")
    pages = own_ref.shape[1]
    half = tokens // 2
    table = table_ref[...]
    request = lax.broadcasted_iota(jnp.int32, table.shape, 0)
    listed = lax.broadcasted_iota(jnp.int32, table.shape, 1)
    lane = lax.broadcasted_iota(jnp.int32, (half, LANES), 1)
    row = lax.broadcasted_iota(jnp.int32, (half, LANES), 0)
    low = (lane % 64) < 32
    inside = row + (lane // 64) * half + (head * share + chunk * tokens)
    for page in range(pages):
        hit = table == me * pages + page
        slot = jnp.sum(jnp.where(hit, listed, 0))
        group = dest_ref[jnp.sum(jnp.where(hit, request, 0))]

        def total(lo, hi, page=page):
            value = own_ref[0, page, lo:hi]
            for term in terms:
                value = value + term[page, lo:hi]
            return value

        parts = [total(b * tokens, (b + 1) * tokens) for b in range(blocks)]
        square = parts[0] * parts[0]
        for part in parts[1:]:
            square = square + part * part
        mean = jnp.sum(square, axis=1, keepdims=True) * (1.0 / (blocks * LANES))
        inverse = lax.rsqrt(mean + EPS)
        scaled = [(part * inverse * gain_ref[b : b + 1]).astype(BF16) for b, part in enumerate(parts)]
        raw = total(blocks * tokens, blocks * tokens + half).astype(BF16).astype(F32)
        other = jnp.where(low, -pltpu.roll(raw, LANES - 32, 1), pltpu.roll(raw, 32, 1))
        angle = freq_ref[...] * (inside + slot * PAGE).astype(F32)
        turned = raw * jnp.cos(angle) + other * jnp.sin(angle)
        page_ref[page, : blocks * tokens] = jnp.concatenate(scaled, axis=0)
        page_ref[page, blocks * tokens :] = turned.astype(BF16)
        place = lax.bitwise_xor(group // 2, me // 2)
        same = group % 2 == me % 2

        @pl.when(same)
        def _(page=page, place=place):
            outs[0][place] = page_ref[page]

        @pl.when(jnp.logical_not(same))
        def _(page=page, place=place):
            outs[1][place] = page_ref[page]


def finish(dest, table, gain, freq, own, terms, tokens, chunk, share):
    _, pages, rows, _ = own.shape
    blocks = gain.shape[0]
    vmem = pl.BlockSpec(memory_space=pltpu.VMEM)
    half_groups = max(dest.shape[0] // 2, 1)
    return pl.pallas_call(
        functools.partial(finish_kernel, tokens=tokens, blocks=blocks, chunk=chunk, share=share),
        in_specs=[pl.BlockSpec(memory_space=pltpu.SMEM)] + [vmem] * (4 + len(terms)),
        out_specs=[vmem] * 2,
        out_shape=[jax.ShapeDtypeStruct((half_groups, rows, LANES), BF16)] * 2,
        scratch_shapes=[pltpu.VMEM((pages, rows, LANES), BF16)],
        compiler_params=params(8),
    )(dest, table, gain, freq, own, *terms)


def select_kernel(dest_ref, table_ref, in_ref, out_ref, *, pages):
    me = lax.axis_index("tok")
    request = request_of(dest_ref, me)
    first = table_ref[request, 0]
    for slot in range(out_ref.shape[0]):
        listed = table_ref[request, slot]
        source = lax.div(jnp.where(listed >= 0, listed, first), pages)
        place = lax.bitwise_xor(lax.div(source, 2), lax.div(me, 2))
        out_ref[slot] = in_ref[place, lax.rem(source + me, 2)]


def select(dest, table, arrived, pages):
    vmem, smem = pl.BlockSpec(memory_space=pltpu.VMEM), pl.BlockSpec(memory_space=pltpu.SMEM)
    return pl.pallas_call(
        functools.partial(select_kernel, pages=pages),
        in_specs=[smem, smem, vmem],
        out_specs=vmem,
        out_shape=jax.ShapeDtypeStruct((table.shape[1],) + arrived.shape[2:], BF16),
        compiler_params=params(8),
    )(dest, table, arrived)


def fold(value, op):
    width = value.shape[1]
    while width > LANES and width % (2 * LANES) == 0:
        width //= 2
        value = op(value[:, :width], value[:, width:])
    return value


def attend_kernel(
    dest_ref, len_ref, q_ref, w_ref, *refs, planes, chunks, tokens, blocks, rows_q, step
):
    payloads = refs[: planes * chunks]
    outs = refs[planes * chunks : planes * (chunks + 1)]
    key_ref, score_ref, acc_ref, top_ref, sum_ref, map_ref, w_buf, w_sem = refs[planes * (chunks + 1) :]
    w_copy = pltpu.make_async_copy(w_ref, w_buf, w_sem)
    w_copy.start()
    head = lax.axis_index("head")
    context = len_ref[request_of(dest_ref, lax.axis_index("tok"))]
    share = tokens * chunks
    width = blocks * LANES
    count = q_ref.shape[0]
    steps = lax.div(context + (step - 1), step)
    live = steps * (step // PAGE)

    for plane in range(planes):
        for chunk in range(chunks):
            payload = payloads[plane * chunks + chunk]
            offset = lax.rem(head + (planes - plane), planes) * share + chunk * tokens

            def fill(slot, _, payload=payload, offset=offset):
                at = pl.multiple_of(slot * PAGE + offset, tokens)
                for b in range(blocks):
                    key_ref[pl.ds(at, tokens), b * LANES : (b + 1) * LANES] = payload[
                        slot, b * tokens : (b + 1) * tokens
                    ]
                packed = payload[slot, width * tokens // LANES :].astype(F32)
                swapped = pltpu.roll(packed, 64, 1)
                key_ref[pl.ds(at, tokens), width:] = jnp.concatenate([packed, swapped], axis=0).astype(BF16)
                return 0

            lax.fori_loop(0, live, fill, 0)

    top_ref[...] = jnp.full_like(top_ref, FLOOR)

    def score_step(i, _):
        at = pl.multiple_of(i * step, step)
        scores = nt_dot(q_ref[...], key_ref[pl.ds(at, step)])
        position = at + lax.broadcasted_iota(jnp.int32, (1, step), 1)
        scores = scores + jnp.where(position < context, 0.0, FLOOR)
        score_ref[i] = scores
        top_ref[...] = jnp.maximum(top_ref[...], fold(scores, jnp.maximum))
        return 0

    lax.fori_loop(0, steps, score_step, 0)
    top = jnp.max(top_ref[...], axis=1, keepdims=True)
    acc_ref[...] = jnp.zeros_like(acc_ref)
    sum_ref[...] = jnp.zeros_like(sum_ref)

    def value_step(i, _):
        at = pl.multiple_of(i * step, step)
        weights = jnp.exp2((score_ref[i] - top) * (SCALE * LOG2E))
        acc_ref[...] += jnp.dot(
            weights.astype(BF16), key_ref[pl.ds(at, step), :width], preferred_element_type=F32
        )
        sum_ref[...] += fold(weights, jnp.add)
        return 0

    lax.fori_loop(0, steps, value_step, 0)
    owned = rows_q // planes
    inverse = 1.0 / jnp.sum(sum_ref[...], axis=1, keepdims=True)
    w_copy.wait()
    for h in range(count // rows_q):
        rows = slice(h * rows_q, (h + 1) * rows_q)
        attended = (acc_ref[rows] * inverse[rows]).astype(BF16)
        mapped = jnp.dot(attended, w_buf[h], preferred_element_type=F32)
        for p in range(planes):
            map_ref[p, :, h * LANES : (h + 1) * LANES] = mapped[p * owned : (p + 1) * owned]
    for d in range(planes):
        outs[d][...] = map_ref[lax.rem(head + d, planes)].astype(BF16)


def attend(dest, ctx_len, query, w_value, payloads, planes, chunks, tokens):
    heads, lat, _ = w_value.shape
    count = query.shape[0]
    rows_q = count // heads
    slots = payloads[0].shape[0]
    step = 2 * PAGE if slots % 2 == 0 else PAGE
    keys = slots * PAGE
    vmem, smem = pl.BlockSpec(memory_space=pltpu.VMEM), pl.BlockSpec(memory_space=pltpu.SMEM)
    return pl.pallas_call(
        functools.partial(
            attend_kernel,
            planes=planes,
            chunks=chunks,
            tokens=tokens,
            blocks=lat // LANES,
            rows_q=rows_q,
            step=step,
        ),
        in_specs=[smem, smem, vmem, pl.BlockSpec(memory_space=pltpu.HBM)] + [vmem] * len(payloads),
        out_specs=[vmem] * planes,
        out_shape=[jax.ShapeDtypeStruct((rows_q // planes, heads * LANES), BF16)] * planes,
        scratch_shapes=[
            pltpu.VMEM((keys, lat + LANES), BF16),
            pltpu.VMEM((keys // step, count, step), F32),
            pltpu.VMEM((count, lat), F32),
            pltpu.VMEM((count, LANES), F32),
            pltpu.VMEM((count, LANES), F32),
            pltpu.VMEM((planes, rows_q // planes, heads * LANES), F32),
            pltpu.VMEM(w_value.shape, BF16),
            pltpu.SemaphoreType.DMA,
        ],
        compiler_params=params(60),
    )(dest, ctx_len, query, w_value, *payloads)


def shift(value, axis, by):
    count = lax.axis_size(axis)
    return lax.ppermute(value, axis, [(i, (i + by) % count) for i in range(count)])


def trade(value, mask):
    count = lax.axis_size("tok")
    return lax.ppermute(value, "tok", [(i, i ^ mask) for i in range(count)])


CHUNKS = 2


def run_device(
    hidden, w_latent, w_rope, kv_gain, q_latent, q_rope, w_value, page_table, dest_group, ctx_len
):
    groups, planes = lax.axis_size("tok"), lax.axis_size("head")
    my_head = lax.axis_index("head")
    pages = hidden.shape[0] // PAGE
    share = PAGE // planes
    chunks = CHUNKS if share // CHUNKS >= 16 else 1
    tokens = share // chunks
    blocks = w_latent.shape[1] // LANES
    rope_width = w_rope.shape[1]

    others = (my_head + 1 + jnp.arange(planes - 1, dtype=jnp.int32)) % planes
    sent = project(hidden, w_latent, w_rope, others.astype(jnp.int32), planes, chunks)
    arrived = []
    for c in range(chunks):
        arrived.append([shift(sent[c][d - 1], "head", d) for d in range(1, planes)])
    own = project(hidden, w_latent, w_rope, my_head[None].astype(jnp.int32), planes, chunks)

    rows_q, heads = q_latent.shape[1], q_latent.shape[2]
    query_side = q_rope[0].reshape(rows_q, heads, rope_width)
    query_side = jnp.pad(query_side, ((0, 0), (0, 0), (0, LANES - rope_width)))
    query = jnp.concatenate([q_latent[0], query_side], axis=2).transpose(1, 0, 2)
    query = query.reshape(heads * rows_q, -1)

    half_width = rope_width // 2
    freq = np.power(THETA, -2.0 * np.arange(half_width) / rope_width)
    freq = jnp.asarray(np.tile(freq, LANES // half_width)[None].astype(np.float32))
    gain = kv_gain.reshape(blocks, LANES)

    picked = []
    for c in range(chunks):
        mine, other = finish(
            dest_group, page_table, gain, freq, own[c], arrived[c], tokens, c, share
        )
        got = trade(other, 1)
        landed = [jnp.stack([mine[0], got[0]])]
        for k in range(1, groups // 2):
            landed.append(trade(jnp.stack([mine[k], got[k]]), 2 * k))
        picked.append(select(dest_group, page_table, jnp.stack(landed), pages))
    payloads = list(picked)
    for d in range(1, planes):
        for c in range(chunks):
            payloads.append(shift(picked[c], "head", d))
    mapped = attend(dest_group, ctx_len, query, w_value, payloads, planes, chunks, tokens)

    pieces = [mapped[0]] + [shift(mapped[d], "head", d) for d in range(1, planes)]
    columns = []
    for source in range(planes):
        behind = (my_head - source) % planes
        column = pieces[0]
        for d in range(1, planes):
            column = jnp.where(behind == d, pieces[d], column)
        columns.append(column)
    return jnp.concatenate(columns, axis=1)[None]


def solution(mesh):
    placed = (
        P("tok", "head"),
        P("head", None),
        P("head", None),
        P(),
        P("tok", None, "head", None),
        P("tok", None, "head"),
        P("head", None, None),
        P(),
        P(),
        P(),
    )
    return jax.shard_map(
        run_device, mesh=mesh, in_specs=placed, out_specs=P("tok", "head", None), check_vma=False
    )
```

```python
import functools

import jax
import jax.numpy as jnp
import numpy as np
from jax import lax
from jax.experimental import pallas as pl
from jax.experimental.pallas import tpu as pltpu
from jax.sharding import PartitionSpec as P


PAGE = 128
LANES = 128
EPS = 1e-06
SCALE = 192.0 ** (-0.5)
THETA = 10000.0
LOG2E = 1.4426950408889634
FLOOR = -1e30
BF16, F32 = jnp.bfloat16, jnp.float32


MIB = 1024 * 1024
PART_MIB, END_MIB = 24, 24


def params(mib):
    return pltpu.CompilerParams(vmem_limit_bytes=mib * MIB)


def nt_dot(a, b):
    return lax.dot_general(a, b, (((1,), (1,)), ((), ())), preferred_element_type=F32)


def project_kernel(
    share_ref, hid_ref, wl_ref, wr_ref, *refs, chunks, pages, tokens, parts, shares
):
    outs, (hid_buf, wl_buf, wr_buf, sems) = refs[:chunks], refs[chunks:]
    share = tokens * chunks
    half = tokens // 2
    depth = hid_ref.shape[-1] // parts
    copies = []
    for k in range(parts):
        at = pl.ds(k * depth, depth)
        copies.append(
            [
                pltpu.make_async_copy(wl_ref.at[at], wl_buf.at[at], sems.at[0, k]),
                pltpu.make_async_copy(wr_ref.at[:, at], wr_buf.at[:, at], sems.at[1, k]),
            ]
            + [
                pltpu.make_async_copy(
                    hid_ref.at[:, share_ref[s], :, at], hid_buf.at[s, :, :, at], sems.at[2 + s, k]
                )
                for s in range(shares)
            ]
        )
    for group in copies:
        for copy in group:
            copy.start()
    for s in range(shares):
        lat = rope = None
        for k in range(parts):
            for copy in copies[k] if s == 0 else ():
                copy.wait()
            rows = hid_buf[s, :, :, k * depth : (k + 1) * depth].reshape(pages * share, depth)
            wide = jnp.dot(rows, wl_buf[k * depth : (k + 1) * depth], preferred_element_type=F32)
            side = nt_dot(rows, wr_buf[:, k * depth : (k + 1) * depth])
            lat, rope = (wide, side) if k == 0 else (lat + wide, rope + side)
        blocks = lat.shape[1] // LANES
        for page in range(pages):
            for c in range(chunks):
                at = (page * chunks + c) * tokens
                for b in range(blocks):
                    outs[c][s, page, b * tokens : (b + 1) * tokens] = lat[
                        at : at + tokens, b * LANES : (b + 1) * LANES
                    ]
                outs[c][s, page, blocks * tokens :] = jnp.concatenate(
                    [rope[at : at + half], rope[at + half : at + tokens]], axis=1
                )


def project(hidden, w_latent, w_rope, shares, head_count, chunks, keep=False):
    features = hidden.shape[1]
    pages = hidden.shape[0] // PAGE
    share = PAGE // head_count
    tokens = share // chunks
    parts = next(n for n in (5, 4, 2, 1) if features % (n * LANES) == 0)
    rows = tokens * (w_latent.shape[1] // LANES) + tokens // 2
    count = shares.shape[0]
    view = hidden.reshape(pages, head_count, share, features)
    side = w_rope.T
    hbm = pl.BlockSpec(memory_space=pltpu.HBM)
    flops = 2 * count * pages * share * features * (w_latent.shape[1] + w_rope.shape[1])
    return pl.pallas_call(
        functools.partial(
            project_kernel, chunks=chunks, pages=pages, tokens=tokens, parts=parts, shares=count
        ),
        in_specs=[pl.BlockSpec(memory_space=pltpu.SMEM), hbm, hbm, hbm],
        out_specs=[pl.BlockSpec(memory_space=pltpu.VMEM)] * chunks,
        out_shape=[jax.ShapeDtypeStruct((count, pages, rows, LANES), F32)] * chunks,
        scratch_shapes=[
            pltpu.VMEM((count, pages, share, features), BF16),
            pltpu.VMEM(w_latent.shape, BF16),
            pltpu.VMEM(side.shape, BF16),
            pltpu.SemaphoreType.DMA((2 + count, parts)),
        ],
        compiler_params=params(63 if count > 1 or not keep else 62),
        cost_estimate=pl.CostEstimate(
            flops=flops,
            bytes_accessed=2 * features * (count * pages * share + w_latent.shape[1] + LANES),
            transcendentals=0,
        ),
    )(shares, view, w_latent, side)


def request_of(dest_ref, group):
    def look(i, found):
        return jnp.where(dest_ref[i] == group, i, found)

    return lax.fori_loop(0, dest_ref.shape[0], look, 0)


def finish_kernel(dest_ref, table_ref, gain_ref, freq_ref, own_ref, *refs, tokens, blocks, chunk, share):
    terms, outs, page_ref = refs[:-3], refs[-3:-1], refs[-1]
    me, head = lax.axis_index("tok"), lax.axis_index("head")
    pages = own_ref.shape[1]
    half = tokens // 2
    table = table_ref[...]
    request = lax.broadcasted_iota(jnp.int32, table.shape, 0)
    listed = lax.broadcasted_iota(jnp.int32, table.shape, 1)
    lane = lax.broadcasted_iota(jnp.int32, (half, LANES), 1)
    row = lax.broadcasted_iota(jnp.int32, (half, LANES), 0)
    low = (lane % 64) < 32
    inside = row + (lane // 64) * half + (head * share + chunk * tokens)
    for page in range(pages):
        hit = table == me * pages + page
        slot = jnp.sum(jnp.where(hit, listed, 0))
        group = dest_ref[jnp.sum(jnp.where(hit, request, 0))]

        def total(lo, hi, page=page):
            value = own_ref[0, page, lo:hi]
            for term in terms:
                value = value + term[page, lo:hi]
            return value

        parts = [total(b * tokens, (b + 1) * tokens) for b in range(blocks)]
        square = parts[0] * parts[0]
        for part in parts[1:]:
            square = square + part * part
        mean = jnp.sum(square, axis=1, keepdims=True) * (1.0 / (blocks * LANES))
        inverse = lax.rsqrt(mean + EPS)
        scaled = [(part * inverse * gain_ref[b : b + 1]).astype(BF16) for b, part in enumerate(parts)]
        raw = total(blocks * tokens, blocks * tokens + half).astype(BF16).astype(F32)
        other = jnp.where(low, -pltpu.roll(raw, LANES - 32, 1), pltpu.roll(raw, 32, 1))
        angle = freq_ref[...] * (inside + slot * PAGE).astype(F32)
        turned = raw * jnp.cos(angle) + other * jnp.sin(angle)
        page_ref[page, : blocks * tokens] = jnp.concatenate(scaled, axis=0)
        page_ref[page, blocks * tokens :] = turned.astype(BF16)
        place = lax.bitwise_xor(group // 2, me // 2)
        same = group % 2 == me % 2

        @pl.when(same)
        def _(page=page, place=place):
            outs[0][place] = page_ref[page]

        @pl.when(jnp.logical_not(same))
        def _(page=page, place=place):
            outs[1][place] = page_ref[page]


def finish(dest, table, gain, freq, own, terms, tokens, chunk, share):
    _, pages, rows, _ = own.shape
    blocks = gain.shape[0]
    vmem = pl.BlockSpec(memory_space=pltpu.VMEM)
    half_groups = max(dest.shape[0] // 2, 1)
    return pl.pallas_call(
        functools.partial(finish_kernel, tokens=tokens, blocks=blocks, chunk=chunk, share=share),
        in_specs=[pl.BlockSpec(memory_space=pltpu.SMEM)] + [vmem] * (4 + len(terms)),
        out_specs=[vmem] * 2,
        out_shape=[jax.ShapeDtypeStruct((half_groups, rows, LANES), BF16)] * 2,
        scratch_shapes=[pltpu.VMEM((pages, rows, LANES), BF16)],
        compiler_params=params(8),
    )(dest, table, gain, freq, own, *terms)


def select_kernel(dest_ref, table_ref, in_ref, out_ref, *, pages):
    me = lax.axis_index("tok")
    request = request_of(dest_ref, me)
    first = table_ref[request, 0]
    for slot in range(out_ref.shape[0]):
        listed = table_ref[request, slot]
        source = lax.div(jnp.where(listed >= 0, listed, first), pages)
        place = lax.bitwise_xor(lax.div(source, 2), lax.div(me, 2))
        out_ref[slot] = in_ref[place, lax.rem(source + me, 2)]


def select(dest, table, arrived, pages):
    vmem, smem = pl.BlockSpec(memory_space=pltpu.VMEM), pl.BlockSpec(memory_space=pltpu.SMEM)
    return pl.pallas_call(
        functools.partial(select_kernel, pages=pages),
        in_specs=[smem, smem, vmem],
        out_specs=vmem,
        out_shape=jax.ShapeDtypeStruct((table.shape[1],) + arrived.shape[2:], BF16),
        compiler_params=params(8),
    )(dest, table, arrived)


def fold(value, op):
    parts = [value[:, at : at + LANES] for at in range(0, value.shape[1], LANES)]
    while len(parts) > 1:
        pairs = [op(x, y) for x, y in zip(parts[::2], parts[1::2])]
        parts = pairs + parts[len(pairs) * 2 :]
    return parts[0]


def fill_keys(key_ref, payloads, tokens, width):
    region = payloads[0].shape[0] * tokens
    for n, payload in enumerate(payloads):
        def fill(slot, _, n=n, payload=payload):
            at = pl.multiple_of(n * region + slot * tokens, tokens)
            for b in range(width // LANES):
                key_ref[pl.ds(at, tokens), b * LANES : (b + 1) * LANES] = payload[
                    slot, b * tokens : (b + 1) * tokens
                ]
            packed = payload[slot, width * tokens // LANES :].astype(F32)
            swapped = pltpu.roll(packed, 64, 1)
            key_ref[pl.ds(at, tokens), width:] = jnp.concatenate([packed, swapped], axis=0).astype(BF16)
            return 0

        lax.fori_loop(0, payload.shape[0], fill, 0)
    used = len(payloads) * region
    if used < key_ref.shape[0]:
        key_ref[used:] = jnp.zeros_like(key_ref[used:])


def dead_bias(at, step, context, slots, tokens, offsets):
    row = at + lax.broadcasted_iota(jnp.int32, (1, step), 1)
    region = slots * tokens
    position = jnp.full((1, step), slots * PAGE, jnp.int32)
    for n, offset in enumerate(offsets):
        rest = row - n * region
        inside = (rest // tokens) * PAGE + offset + rest % tokens
        position = jnp.where((rest >= 0) & (rest < region), inside, position)
    return jnp.where(position < context, 0.0, FLOOR)


def payload_offsets(origins, planes, chunks, tokens):
    head = lax.axis_index("head")
    return [
        lax.rem(head + (planes - behind), planes) * (tokens * chunks) + chunk * tokens
        for behind, chunk in origins
    ]


def score_keys(q_ref, key_ref, score_ref, top_ref, bias_of):
    blocks, _, step = score_ref.shape

    def score_step(i, _):
        at = pl.multiple_of(i * step, step)
        scores = nt_dot(q_ref[...], key_ref[pl.ds(at, step)]) + bias_of(at, step)
        score_ref[i] = scores
        top_ref[...] = jnp.maximum(top_ref[...], fold(scores, jnp.maximum))
        return 0

    lax.fori_loop(0, blocks, score_step, 0)


def weigh_keys(key_ref, score_ref, acc_ref, sum_ref, top, width):
    blocks, _, step = score_ref.shape

    def value_step(i, _):
        at = pl.multiple_of(i * step, step)
        weights = jnp.exp2((score_ref[i] - top) * (SCALE * LOG2E))
        acc_ref[...] += jnp.dot(
            weights.astype(BF16), key_ref[pl.ds(at, step), :width], preferred_element_type=F32
        )
        sum_ref[...] += fold(weights, jnp.add)
        return 0

    lax.fori_loop(0, blocks, value_step, 0)


def start_state(acc_ref, top_ref, sum_ref, carried, top_of):
    if not carried:
        top_ref[...] = jnp.full_like(top_ref, FLOOR)
    else:
        top_ref[...] = carried[1][...]
    top_of()
    top = jnp.max(top_ref[...], axis=1, keepdims=True)
    if not carried:
        acc_ref[...] = jnp.zeros_like(acc_ref)
        sum_ref[...] = jnp.zeros_like(sum_ref)
    else:
        factor = jnp.exp2((carried[1][:, :1] - top) * (SCALE * LOG2E))
        acc_ref[...] = carried[0][...] * factor
        sum_ref[...] = carried[2][...] * factor
    return top


def part_kernel(dest_ref, len_ref, q_ref, *refs, carry, origins, planes, chunks, tokens, width):
    carried, refs = refs[:carry], refs[carry:]
    payloads = refs[: len(origins)]
    acc_ref, top_ref, sum_ref, key_ref, score_ref = refs[len(origins) :]
    context = len_ref[request_of(dest_ref, lax.axis_index("tok"))]
    offsets = payload_offsets(origins, planes, chunks, tokens)
    slots = payloads[0].shape[0]
    fill_keys(key_ref, payloads, tokens, width)
    top = start_state(
        acc_ref, top_ref, sum_ref, carried,
        lambda: score_keys(
            q_ref, key_ref, score_ref, top_ref,
            lambda at, step: dead_bias(at, step, context, slots, tokens, offsets),
        ),
    )
    top_ref[...] = jnp.broadcast_to(top, top_ref.shape)
    weigh_keys(key_ref, score_ref, acc_ref, sum_ref, top, width)


def end_kernel(
    dest_ref, len_ref, q_ref, w_ref, acc0_ref, top0_ref, sum0_ref, *refs,
    origins, planes, chunks, tokens, width, rows_q,
):
    payloads = refs[: len(origins)]
    outs = refs[len(origins) : len(origins) + planes]
    key_ref, score_ref, acc_ref, top_ref, sum_ref, map_ref, w_buf, w_sem = refs[len(origins) + planes :]
    w_copy = pltpu.make_async_copy(w_ref, w_buf, w_sem)
    w_copy.start()
    head = lax.axis_index("head")
    context = len_ref[request_of(dest_ref, lax.axis_index("tok"))]
    offsets = payload_offsets(origins, planes, chunks, tokens)
    slots = payloads[0].shape[0]
    count = q_ref.shape[0]
    fill_keys(key_ref, payloads, tokens, width)
    top = start_state(
        acc_ref, top_ref, sum_ref, (acc0_ref, top0_ref, sum0_ref),
        lambda: score_keys(
            q_ref, key_ref, score_ref, top_ref,
            lambda at, step: dead_bias(at, step, context, slots, tokens, offsets),
        ),
    )
    weigh_keys(key_ref, score_ref, acc_ref, sum_ref, top, width)
    owned = rows_q // planes
    inverse = 1.0 / jnp.sum(sum_ref[...], axis=1, keepdims=True)
    w_copy.wait()
    for h in range(count // rows_q):
        rows = slice(h * rows_q, (h + 1) * rows_q)
        attended = (acc_ref[rows] * inverse[rows]).astype(BF16)
        mapped = jnp.dot(attended, w_buf[h], preferred_element_type=F32)
        for p in range(planes):
            map_ref[p, :, h * LANES : (h + 1) * LANES] = mapped[p * owned : (p + 1) * owned]
    for d in range(planes):
        outs[d][...] = map_ref[lax.rem(head + d, planes)].astype(BF16)


def key_scratch(payloads, tokens, count, lat):
    used = len(payloads) * payloads[0].shape[0] * tokens
    step = 256 if used > 512 else (used + LANES - 1) // LANES * LANES
    keys = (used + step - 1) // step * step
    return [pltpu.VMEM((keys, lat + LANES), BF16), pltpu.VMEM((keys // step, count, step), F32)]


def attend_part(dest, ctx_len, query, lat, payloads, carried, planes, chunks, tokens):
    count = query.shape[0]
    vmem, smem = pl.BlockSpec(memory_space=pltpu.VMEM), pl.BlockSpec(memory_space=pltpu.SMEM)
    state = [(count, lat), (count, LANES), (count, LANES)]
    return pl.pallas_call(
        functools.partial(
            part_kernel,
            carry=len(carried),
            origins=tuple(payloads),
            planes=planes,
            chunks=chunks,
            tokens=tokens,
            width=lat,
        ),
        in_specs=[smem, smem, vmem] + [vmem] * (len(carried) + len(payloads)),
        out_specs=[vmem] * 3,
        out_shape=[jax.ShapeDtypeStruct(shape, F32) for shape in state],
        scratch_shapes=key_scratch(list(payloads.values()), tokens, count, lat),
        compiler_params=params(PART_MIB),
    )(dest, ctx_len, query, *carried, *payloads.values())


def attend_end(dest, ctx_len, query, w_value, payloads, carried, planes, chunks, tokens):
    heads, lat, _ = w_value.shape
    count = query.shape[0]
    rows_q = count // heads
    vmem, smem = pl.BlockSpec(memory_space=pltpu.VMEM), pl.BlockSpec(memory_space=pltpu.SMEM)
    state = [(count, lat), (count, LANES), (count, LANES)]
    return pl.pallas_call(
        functools.partial(
            end_kernel,
            origins=tuple(payloads),
            planes=planes,
            chunks=chunks,
            tokens=tokens,
            width=lat,
            rows_q=rows_q,
        ),
        in_specs=[smem, smem, vmem, pl.BlockSpec(memory_space=pltpu.HBM)] + [vmem] * (3 + len(payloads)),
        out_specs=[vmem] * planes,
        out_shape=[jax.ShapeDtypeStruct((rows_q // planes, heads * LANES), BF16)] * planes,
        scratch_shapes=key_scratch(list(payloads.values()), tokens, count, lat)
        + [pltpu.VMEM(shape, F32) for shape in state]
        + [
            pltpu.VMEM((planes, rows_q // planes, heads * LANES), F32),
            pltpu.VMEM(w_value.shape, BF16),
            pltpu.SemaphoreType.DMA,
        ],
        compiler_params=params(END_MIB),
    )(dest, ctx_len, query, w_value, *carried, *payloads.values())


def place_kernel(*refs):
    out_ref, pieces = refs[-1], refs[:-1]
    head, planes = lax.axis_index("head"), len(pieces)
    width = pieces[0].shape[1]
    for d, piece in enumerate(pieces):
        first = pl.multiple_of(lax.rem(head + (planes - d), planes) * width, width)
        out_ref[:, pl.ds(first, width)] = piece[...]


def place(pieces):
    vmem = pl.BlockSpec(memory_space=pltpu.VMEM)
    rows, width = pieces[0].shape
    return pl.pallas_call(
        place_kernel,
        in_specs=[vmem] * len(pieces),
        out_specs=vmem,
        out_shape=jax.ShapeDtypeStruct((rows, width * len(pieces)), BF16),
        compiler_params=params(8),
    )(*pieces)


def shift(value, axis, by):
    count = lax.axis_size(axis)
    return lax.ppermute(value, axis, [(i, (i + by) % count) for i in range(count)])


def trade(value, mask):
    count = lax.axis_size("tok")
    return lax.ppermute(value, "tok", [(i, i ^ mask) for i in range(count)])


CHUNKS = 2


def run_device(
    hidden, w_latent, w_rope, kv_gain, q_latent, q_rope, w_value, page_table, dest_group, ctx_len
):
    groups, planes = lax.axis_size("tok"), lax.axis_size("head")
    my_head = lax.axis_index("head")
    pages = hidden.shape[0] // PAGE
    share = PAGE // planes
    chunks = CHUNKS if share // CHUNKS >= 16 else 1
    tokens = share // chunks
    blocks = w_latent.shape[1] // LANES
    rope_width = w_rope.shape[1]

    others = (my_head + 1 + jnp.arange(planes - 1, dtype=jnp.int32)) % planes
    sent = project(hidden, w_latent, w_rope, others.astype(jnp.int32), planes, chunks)
    arrived = []
    for c in range(chunks):
        arrived.append([shift(sent[c][d - 1], "head", d) for d in range(1, planes)])
    own = project(hidden, w_latent, w_rope, my_head[None].astype(jnp.int32), planes, chunks, True)

    rows_q, heads = q_latent.shape[1], q_latent.shape[2]
    query_side = q_rope[0].reshape(rows_q, heads, rope_width)
    query_side = jnp.pad(query_side, ((0, 0), (0, 0), (0, LANES - rope_width)))
    query = jnp.concatenate([q_latent[0], query_side], axis=2).transpose(1, 0, 2)
    query = query.reshape(heads * rows_q, -1)

    half_width = rope_width // 2
    freq = np.power(THETA, -2.0 * np.arange(half_width) / rope_width)
    freq = jnp.asarray(np.tile(freq, LANES // half_width)[None].astype(np.float32))
    gain = kv_gain.reshape(blocks, LANES)

    picked = []
    for c in range(chunks):
        mine, other = finish(
            dest_group, page_table, gain, freq, own[c], arrived[c], tokens, c, share
        )
        got = trade(other, 1)
        landed = [jnp.stack([mine[0], got[0]])]
        for k in range(1, groups // 2):
            landed.append(trade(jnp.stack([mine[k], got[k]]), 2 * k))
        picked.append(select(dest_group, page_table, jnp.stack(landed), pages))
    sent_keys = []
    for c in range(chunks):
        sent_keys.append({(d, c): shift(picked[c], "head", d) for d in range(1, planes)})
    carried = ()
    for c in range(chunks):
        local = {(0, c): picked[c], **(sent_keys[c - 1] if c > 0 else {})}
        carried = attend_part(
            dest_group, ctx_len, query, w_value.shape[1], local, carried, planes, chunks, tokens
        )
    mapped = attend_end(
        dest_group, ctx_len, query, w_value, sent_keys[-1], carried, planes, chunks, tokens
    )

    pieces = [mapped[0]] + [shift(mapped[d], "head", d) for d in range(1, planes)]
    return place(pieces)[None]


def solution(mesh):
    placed = (
        P("tok", "head"),
        P("head", None),
        P("head", None),
        P(),
        P("tok", None, "head", None),
        P("tok", None, "head"),
        P("head", None, None),
        P(),
        P(),
        P(),
    )
    return jax.shard_map(
        run_device, mesh=mesh, in_specs=placed, out_specs=P("tok", "head", None), check_vma=False
    )
```

```python
import functools

import jax
import jax.numpy as jnp
import numpy as np
from jax import lax
from jax.experimental import pallas as pl
from jax.experimental.pallas import tpu as pltpu
from jax.sharding import PartitionSpec as P


PAGE = 128
LANES = 128
EPS = 1e-06
SCALE = 192.0 ** (-0.5)
THETA = 10000.0
LOG2E = 1.4426950408889634
FLOOR = -1e30
BF16, F32 = jnp.bfloat16, jnp.float32


MIB = 1024 * 1024
PART_MIB, END_MIB = 24, 24
CUTS = 2


def params(mib):
    return pltpu.CompilerParams(vmem_limit_bytes=mib * MIB)


def nt_dot(a, b):
    return lax.dot_general(a, b, (((1,), (1,)), ((), ())), preferred_element_type=F32)


def project_kernel(share_ref, hid_ref, wl_ref, wr_ref, *refs, which, parts):
    count = len(which)
    outs, (hid_buf, wl_buf, wr_buf, sems) = refs[:count], refs[count:]
    pages, _, _, tokens, features = hid_ref.shape
    half, depth = tokens // 2, features // parts
    copies = []
    for k in range(parts):
        at = pl.ds(k * depth, depth)
        copies.append(
            [
                pltpu.make_async_copy(wl_ref.at[at], wl_buf.at[at], sems.at[0, k]),
                pltpu.make_async_copy(wr_ref.at[:, at], wr_buf.at[:, at], sems.at[1, k]),
            ]
            + [
                pltpu.make_async_copy(
                    hid_ref.at[:, share_ref[n], chunk, :, at], hid_buf.at[n, :, :, at], sems.at[2 + n, k]
                )
                for n, chunk in enumerate(which)
            ]
        )
    for group in copies:
        for copy in group:
            copy.start()
    lat = rope = None
    for k in range(parts):
        for copy in copies[k]:
            copy.wait()
        rows = hid_buf[:, :, :, k * depth : (k + 1) * depth].reshape(count * pages * tokens, depth)
        wide = jnp.dot(rows, wl_buf[k * depth : (k + 1) * depth], preferred_element_type=F32)
        side = nt_dot(rows, wr_buf[:, k * depth : (k + 1) * depth])
        lat, rope = (wide, side) if k == 0 else (lat + wide, rope + side)
    blocks = lat.shape[1] // LANES
    for n in range(count):
        for page in range(pages):
            at = (n * pages + page) * tokens
            for b in range(blocks):
                outs[n][page, b * tokens : (b + 1) * tokens] = lat[
                    at : at + tokens, b * LANES : (b + 1) * LANES
                ]
            outs[n][page, blocks * tokens :] = jnp.concatenate(
                [rope[at : at + half], rope[at + half : at + tokens]], axis=1
            )


def project(hidden, w_latent, w_rope, wanted, planes, chunks, mib):
    features = hidden.shape[1]
    pages = hidden.shape[0] // PAGE
    tokens = PAGE // planes // chunks
    parts = next(n for n in (5, 4, 2, 1) if features % (n * LANES) == 0)
    rows = tokens * (w_latent.shape[1] // LANES) + tokens // 2
    count = len(wanted)
    view = hidden.reshape(pages, planes, chunks, tokens, features)
    shares = sum(
        jnp.where(jnp.arange(count) == n, share, 0) for n, (share, _) in enumerate(wanted)
    ).astype(jnp.int32)
    side = w_rope.T
    hbm = pl.BlockSpec(memory_space=pl.ANY)
    flops = 2 * count * pages * tokens * features * (w_latent.shape[1] + w_rope.shape[1])
    return pl.pallas_call(
        functools.partial(project_kernel, which=tuple(c for _, c in wanted), parts=parts),
        in_specs=[pl.BlockSpec(memory_space=pltpu.SMEM), hbm, hbm, hbm],
        out_specs=[pl.BlockSpec(memory_space=pltpu.VMEM)] * count,
        out_shape=[jax.ShapeDtypeStruct((pages, rows, LANES), F32)] * count,
        scratch_shapes=[
            pltpu.VMEM((count, pages, tokens, features), BF16),
            pltpu.VMEM(w_latent.shape, BF16),
            pltpu.VMEM(side.shape, BF16),
            pltpu.SemaphoreType.DMA((2 + count, parts)),
        ],
        compiler_params=params(mib),
        cost_estimate=pl.CostEstimate(
            flops=flops,
            bytes_accessed=2 * features * (count * pages * tokens + w_latent.shape[1] + LANES),
            transcendentals=0,
        ),
    )(shares, view, w_latent, side)


def request_of(dest_ref, group):
    def look(i, found):
        return jnp.where(dest_ref[i] == group, i, found)

    return lax.fori_loop(0, dest_ref.shape[0], look, 0)


def finish_kernel(dest_ref, table_ref, gain_ref, freq_ref, own_ref, *refs, tokens, blocks, chunk, share):
    terms, outs, page_ref = refs[:-3], refs[-3:-1], refs[-1]
    me, head = lax.axis_index("tok"), lax.axis_index("head")
    pages = own_ref.shape[0]
    half = tokens // 2
    table = table_ref[...]
    request = lax.broadcasted_iota(jnp.int32, table.shape, 0)
    listed = lax.broadcasted_iota(jnp.int32, table.shape, 1)
    lane = lax.broadcasted_iota(jnp.int32, (half, LANES), 1)
    row = lax.broadcasted_iota(jnp.int32, (half, LANES), 0)
    low = (lane % 64) < 32
    inside = row + (lane // 64) * half + (head * share + chunk * tokens)
    hits = [table == me * pages + page for page in range(pages)]
    slots = [jnp.sum(jnp.where(hit, listed, 0)) for hit in hits]
    owners = [jnp.sum(jnp.where(hit, request, 0)) for hit in hits]
    for page in range(pages):

        def total(lo, hi, page=page):
            value = own_ref[page, lo:hi]
            for term in terms:
                value = value + term[page, lo:hi]
            return value

        parts = [total(b * tokens, (b + 1) * tokens) for b in range(blocks)]
        square = parts[0] * parts[0]
        for part in parts[1:]:
            square = square + part * part
        mean = jnp.sum(square, axis=1, keepdims=True) * (1.0 / (blocks * LANES))
        inverse = lax.rsqrt(mean + EPS)
        scaled = [(part * inverse * gain_ref[b : b + 1]).astype(BF16) for b, part in enumerate(parts)]
        raw = total(blocks * tokens, blocks * tokens + half).astype(BF16).astype(F32)
        other = jnp.where(low, -pltpu.roll(raw, LANES - 32, 1), pltpu.roll(raw, 32, 1))
        angle = freq_ref[...] * (inside + slots[page] * PAGE).astype(F32)
        turned = raw * jnp.cos(angle) + other * jnp.sin(angle)
        page_ref[page, : blocks * tokens] = jnp.concatenate(scaled, axis=0)
        page_ref[page, blocks * tokens :] = turned.astype(BF16)
    for page in range(pages):
        group = dest_ref[owners[page]]
        place = lax.bitwise_xor(group // 2, me // 2)
        same = group % 2 == me % 2

        @pl.when(same)
        def _(page=page, place=place):
            outs[0][place] = page_ref[page]

        @pl.when(jnp.logical_not(same))
        def _(page=page, place=place):
            outs[1][place] = page_ref[page]


def finish(dest, table, gain, freq, own, terms, tokens, chunk, share):
    pages, rows, _ = own.shape
    blocks = gain.shape[0]
    vmem = pl.BlockSpec(memory_space=pltpu.VMEM)
    half_groups = max(dest.shape[0] // 2, 1)
    return pl.pallas_call(
        functools.partial(finish_kernel, tokens=tokens, blocks=blocks, chunk=chunk, share=share),
        in_specs=[pl.BlockSpec(memory_space=pltpu.SMEM)] + [vmem] * (4 + len(terms)),
        out_specs=[vmem] * 2,
        out_shape=[jax.ShapeDtypeStruct((half_groups, rows, LANES), BF16)] * 2,
        scratch_shapes=[pltpu.VMEM((pages, rows, LANES), BF16)],
        compiler_params=params(8),
    )(dest, table, gain, freq, own, *terms)


def select_kernel(dest_ref, table_ref, *refs, pages):
    ins, out_ref = refs[:-1], refs[-1]
    me = lax.axis_index("tok")
    request = request_of(dest_ref, me)
    first = table_ref[request, 0]
    for slot in range(out_ref.shape[0]):
        listed = table_ref[request, slot]
        source = lax.div(jnp.where(listed >= 0, listed, first), pages)
        place = lax.bitwise_xor(lax.div(source, 2), lax.div(me, 2))
        if len(ins) == 1:
            out_ref[slot] = ins[0][place, lax.rem(source + me, 2)]
            continue
        same = lax.rem(source + me, 2) == 0

        @pl.when(same)
        def _(slot=slot, place=place):
            out_ref[slot] = ins[0][place]

        @pl.when(jnp.logical_not(same))
        def _(slot=slot, place=place):
            out_ref[slot] = ins[1][place]


def select(dest, table, landed, pages):
    vmem, smem = pl.BlockSpec(memory_space=pltpu.VMEM), pl.BlockSpec(memory_space=pltpu.SMEM)
    return pl.pallas_call(
        functools.partial(select_kernel, pages=pages),
        in_specs=[smem, smem] + [vmem] * len(landed),
        out_specs=vmem,
        out_shape=jax.ShapeDtypeStruct((table.shape[1],) + landed[0].shape[-2:], BF16),
        compiler_params=params(8),
    )(dest, table, *landed)


def fold(value, op):
    parts = [value[:, at : at + LANES] for at in range(0, value.shape[1], LANES)]
    while len(parts) > 1:
        pairs = [op(x, y) for x, y in zip(parts[::2], parts[1::2])]
        parts = pairs + parts[len(pairs) * 2 :]
    return parts[0]


def fill_keys(key_ref, payloads, tokens, width):
    region = payloads[0].shape[0] * tokens
    for n, payload in enumerate(payloads):
        def fill(slot, _, n=n, payload=payload):
            at = pl.multiple_of(n * region + slot * tokens, tokens)
            for b in range(width // LANES):
                key_ref[pl.ds(at, tokens), b * LANES : (b + 1) * LANES] = payload[
                    slot, b * tokens : (b + 1) * tokens
                ]
            packed = payload[slot, width * tokens // LANES :].astype(F32)
            swapped = pltpu.roll(packed, 64, 1)
            key_ref[pl.ds(at, tokens), width:] = jnp.concatenate([packed, swapped], axis=0).astype(BF16)
            return 0

        lax.fori_loop(0, payload.shape[0], fill, 0)
    used = len(payloads) * region
    if used < key_ref.shape[0]:
        key_ref[used:] = jnp.zeros_like(key_ref[used:])


def dead_bias(at, step, context, slots, tokens, offsets):
    row = at + lax.broadcasted_iota(jnp.int32, (1, step), 1)
    region = slots * tokens
    position = jnp.full((1, step), slots * PAGE, jnp.int32)
    for n, offset in enumerate(offsets):
        rest = row - n * region
        inside = (rest // tokens) * PAGE + offset + rest % tokens
        position = jnp.where((rest >= 0) & (rest < region), inside, position)
    return jnp.where(position < context, 0.0, FLOOR)


def payload_offsets(origins, planes, chunks, tokens):
    head = lax.axis_index("head")
    return [
        lax.rem(head + (planes - behind), planes) * (tokens * chunks) + chunk * tokens
        for behind, chunk in origins
    ]


def score_keys(q_ref, key_ref, score_ref, top_ref, bias_of):
    blocks, _, step = score_ref.shape

    def score_step(i, _):
        at = pl.multiple_of(i * step, step)
        scores = nt_dot(q_ref[...], key_ref[pl.ds(at, step)]) + bias_of(at, step)
        score_ref[i] = scores
        top_ref[...] = jnp.maximum(top_ref[...], fold(scores, jnp.maximum))
        return 0

    lax.fori_loop(0, blocks, score_step, 0)


def weigh_keys(key_ref, score_ref, acc_ref, sum_ref, top, width):
    blocks, _, step = score_ref.shape

    def value_step(i, _):
        at = pl.multiple_of(i * step, step)
        weights = jnp.exp2((score_ref[i] - top) * (SCALE * LOG2E))
        acc_ref[...] += jnp.dot(
            weights.astype(BF16), key_ref[pl.ds(at, step), :width], preferred_element_type=F32
        )
        sum_ref[...] += fold(weights, jnp.add)
        return 0

    lax.fori_loop(0, blocks, value_step, 0)


def start_state(acc_ref, top_ref, sum_ref, carried, top_of):
    if not carried:
        top_ref[...] = jnp.full_like(top_ref, FLOOR)
    else:
        top_ref[...] = carried[1][...]
    top_of()
    top = jnp.max(top_ref[...], axis=1, keepdims=True)
    if not carried:
        acc_ref[...] = jnp.zeros_like(acc_ref)
        sum_ref[...] = jnp.zeros_like(sum_ref)
    else:
        factor = jnp.exp2((carried[1][:, :1] - top) * (SCALE * LOG2E))
        acc_ref[...] = carried[0][...] * factor
        sum_ref[...] = carried[2][...] * factor
    return top


def part_kernel(dest_ref, len_ref, q_ref, *refs, carry, origins, planes, chunks, tokens, width):
    carried, refs = refs[:carry], refs[carry:]
    payloads = refs[: len(origins)]
    acc_ref, top_ref, sum_ref, key_ref, score_ref = refs[len(origins) :]
    context = len_ref[request_of(dest_ref, lax.axis_index("tok"))]
    offsets = payload_offsets(origins, planes, chunks, tokens)
    slots = payloads[0].shape[0]
    fill_keys(key_ref, payloads, tokens, width)
    top = start_state(
        acc_ref, top_ref, sum_ref, carried,
        lambda: score_keys(
            q_ref, key_ref, score_ref, top_ref,
            lambda at, step: dead_bias(at, step, context, slots, tokens, offsets),
        ),
    )
    top_ref[...] = jnp.broadcast_to(top, top_ref.shape)
    weigh_keys(key_ref, score_ref, acc_ref, sum_ref, top, width)


def end_kernel(
    dest_ref, len_ref, q_ref, w_ref, acc_ref, top_ref, sum_ref, *refs,
    origins, planes, chunks, tokens, width, rows_q, cuts,
):
    payloads = refs[: len(origins)]
    outs = refs[len(origins) : len(origins) + planes]
    key_ref, score_ref, map_ref, w_buf, w_sem = refs[len(origins) + planes :]
    w_copy = pltpu.make_async_copy(w_ref, w_buf, w_sem)
    w_copy.start()
    head = lax.axis_index("head")
    context = len_ref[request_of(dest_ref, lax.axis_index("tok"))]
    offsets = payload_offsets(origins, planes, chunks, tokens)
    fill_keys(key_ref, payloads, tokens, width)
    blocks, _, step = score_ref.shape
    owned = rows_q // planes
    part = q_ref.shape[0] // cuts
    biases = [
        dead_bias(i * step, step, context, payloads[0].shape[0], tokens, offsets) for i in range(blocks)
    ]
    for cut in range(cuts):
        rows = slice(cut * part, (cut + 1) * part)
        scores = [
            nt_dot(q_ref[rows], key_ref[i * step : (i + 1) * step]) + biases[i] for i in range(blocks)
        ]
        peak = functools.reduce(jnp.maximum, [fold(x, jnp.maximum) for x in scores])
        before = top_ref[rows]
        top = jnp.maximum(jnp.max(peak, axis=1, keepdims=True), before[:, :1])
        factor = jnp.exp2((before[:, :1] - top) * (SCALE * LOG2E))
        weights = [jnp.exp2((x - top) * (SCALE * LOG2E)) for x in scores]
        total = functools.reduce(jnp.add, [fold(x, jnp.add) for x in weights]) + sum_ref[rows] * factor
        inverse = 1.0 / jnp.sum(total, axis=1, keepdims=True)
        summed = acc_ref[rows] * factor
        for i, x in enumerate(weights):
            summed += jnp.dot(
                x.astype(BF16), key_ref[i * step : (i + 1) * step, :width], preferred_element_type=F32
            )
        attended = (summed * inverse).astype(BF16)
        if cut == 0:
            w_copy.wait()
        for h in range(part // rows_q):
            at = cut * (part // rows_q) + h
            mapped = jnp.dot(
                attended[h * rows_q : (h + 1) * rows_q], w_buf[at], preferred_element_type=F32
            )
            for p in range(planes):
                map_ref[p, :, at * LANES : (at + 1) * LANES] = mapped[p * owned : (p + 1) * owned]
    for d in range(planes):
        outs[d][...] = map_ref[lax.rem(head + d, planes)].astype(BF16)


def key_scratch(payloads, tokens, count, lat):
    used = len(payloads) * payloads[0].shape[0] * tokens
    step = 256 if used > 512 else (used + LANES - 1) // LANES * LANES
    keys = (used + step - 1) // step * step
    return [pltpu.VMEM((keys, lat + LANES), BF16), pltpu.VMEM((keys // step, count, step), F32)]


def attend_part(dest, ctx_len, query, lat, payloads, carried, planes, chunks, tokens):
    count = query.shape[0]
    vmem, smem = pl.BlockSpec(memory_space=pltpu.VMEM), pl.BlockSpec(memory_space=pltpu.SMEM)
    state = [(count, lat), (count, LANES), (count, LANES)]
    return pl.pallas_call(
        functools.partial(
            part_kernel,
            carry=len(carried),
            origins=tuple(payloads),
            planes=planes,
            chunks=chunks,
            tokens=tokens,
            width=lat,
        ),
        in_specs=[smem, smem, vmem] + [vmem] * (len(carried) + len(payloads)),
        out_specs=[vmem] * 3,
        out_shape=[jax.ShapeDtypeStruct(shape, F32) for shape in state],
        scratch_shapes=key_scratch(list(payloads.values()), tokens, count, lat),
        compiler_params=params(PART_MIB),
    )(dest, ctx_len, query, *carried, *payloads.values())


def attend_end(dest, ctx_len, query, w_value, payloads, carried, planes, chunks, tokens):
    heads, lat, _ = w_value.shape
    count = query.shape[0]
    rows_q = count // heads
    vmem, smem = pl.BlockSpec(memory_space=pltpu.VMEM), pl.BlockSpec(memory_space=pltpu.SMEM)
    return pl.pallas_call(
        functools.partial(
            end_kernel,
            origins=tuple(payloads),
            planes=planes,
            chunks=chunks,
            tokens=tokens,
            width=lat,
            rows_q=rows_q,
            cuts=CUTS if heads % CUTS == 0 else 1,
        ),
        in_specs=[smem, smem, vmem, pl.BlockSpec(memory_space=pltpu.HBM)] + [vmem] * (3 + len(payloads)),
        out_specs=[vmem] * planes,
        out_shape=[jax.ShapeDtypeStruct((rows_q // planes, heads * LANES), BF16)] * planes,
        scratch_shapes=key_scratch(list(payloads.values()), tokens, count, lat)
        + [
            pltpu.VMEM((planes, rows_q // planes, heads * LANES), F32),
            pltpu.VMEM(w_value.shape, BF16),
            pltpu.SemaphoreType.DMA,
        ],
        compiler_params=params(END_MIB),
    )(dest, ctx_len, query, w_value, *carried, *payloads.values())


def place_kernel(*refs):
    out_ref, pieces = refs[-1], refs[:-1]
    head, planes = lax.axis_index("head"), len(pieces)
    width = pieces[0].shape[1]
    for d, piece in enumerate(pieces):
        first = pl.multiple_of(lax.rem(head + (planes - d), planes) * width, width)
        out_ref[:, pl.ds(first, width)] = piece[...]


def place(pieces):
    vmem = pl.BlockSpec(memory_space=pltpu.VMEM)
    rows, width = pieces[0].shape
    return pl.pallas_call(
        place_kernel,
        in_specs=[vmem] * len(pieces),
        out_specs=vmem,
        out_shape=jax.ShapeDtypeStruct((rows, width * len(pieces)), BF16),
        compiler_params=params(8),
    )(*pieces)


def shift(value, axis, by):
    count = lax.axis_size(axis)
    return lax.ppermute(value, axis, [(i, (i + by) % count) for i in range(count)])


def trade(value, mask):
    count = lax.axis_size("tok")
    return lax.ppermute(value, "tok", [(i, i ^ mask) for i in range(count)])


CHUNKS = 2


def run_device(
    hidden, w_latent, w_rope, kv_gain, q_latent, q_rope, w_value, page_table, dest_group, ctx_len
):
    groups, planes = lax.axis_size("tok"), lax.axis_size("head")
    my_head = lax.axis_index("head")
    pages = hidden.shape[0] // PAGE
    share = PAGE // planes
    chunks = CHUNKS if share // CHUNKS >= 16 else 1
    tokens = share // chunks
    blocks = w_latent.shape[1] // LANES
    rope_width = w_rope.shape[1]

    others = [(my_head + d) % planes for d in range(1, planes)]
    sent = project(hidden, w_latent, w_rope, [(o, 0) for o in others], planes, chunks, 63)
    rest = [(o, c) for c in range(1, chunks) for o in others] + [(my_head, c) for c in range(chunks)]
    rest = project(hidden, w_latent, w_rope, rest, planes, chunks, 58)
    sent, own = list(sent) + list(rest[:-chunks]), rest[-chunks:]
    arrived = []
    for c in range(chunks):
        arrived.append(
            [shift(sent[c * (planes - 1) + d - 1], "head", d) for d in range(1, planes)]
        )

    rows_q, heads = q_latent.shape[1], q_latent.shape[2]
    query_side = q_rope[0].reshape(rows_q, heads, rope_width)
    query_side = jnp.pad(query_side, ((0, 0), (0, 0), (0, LANES - rope_width)))
    query = jnp.concatenate([q_latent[0], query_side], axis=2).transpose(1, 0, 2)
    query = query.reshape(heads * rows_q, -1)

    half_width = rope_width // 2
    freq = np.power(THETA, -2.0 * np.arange(half_width) / rope_width)
    freq = jnp.asarray(np.tile(freq, LANES // half_width)[None].astype(np.float32))
    gain = kv_gain.reshape(blocks, LANES)

    picked = []
    for c in range(chunks):
        mine, other = finish(
            dest_group, page_table, gain, freq, own[c], arrived[c], tokens, c, share
        )
        late = c == 0
        if not late:
            other = trade(other, 1)
        landed = [jnp.stack([mine[0], other[0]])]
        for k in range(1, groups // 2):
            landed.append(trade(jnp.stack([mine[k], other[k]]), 2 * k))
        if late:
            crossed = trade(jnp.stack([x[1] for x in landed]), 1)
            landed = [jnp.stack([x[0] for x in landed]), crossed]
        else:
            landed = [jnp.stack(landed)]
        picked.append(select(dest_group, page_table, landed, pages))
    sent_keys = []
    for c in range(chunks):
        sent_keys.append({(d, c): shift(picked[c], "head", d) for d in range(1, planes)})
    carried = ()
    for c in range(chunks):
        local = {(0, c): picked[c], **(sent_keys[c - 1] if c > 0 else {})}
        carried = attend_part(
            dest_group, ctx_len, query, w_value.shape[1], local, carried, planes, chunks, tokens
        )
    mapped = attend_end(
        dest_group, ctx_len, query, w_value, sent_keys[-1], carried, planes, chunks, tokens
    )

    pieces = [mapped[0]] + [shift(mapped[d], "head", d) for d in range(1, planes)]
    return place(pieces)[None]


def solution(mesh):
    placed = (
        P("tok", "head"),
        P("head", None),
        P("head", None),
        P(),
        P("tok", None, "head", None),
        P("tok", None, "head"),
        P("head", None, None),
        P(),
        P(),
        P(),
    )
    return jax.shard_map(run_device, mesh=mesh, in_specs=placed, out_specs=P("tok", "head", None), check_vma=False)
```
